512 devices in a mesh: row: 64 (over y, z), col: 8 (over x, core).
Axes of the slice: x: 4, y: 4, z: 16, core: 2. Of those that a mesh axis runs over, the one named last changes fastest.
Arguments:
- kernel: bfloat16 [328, 64, 8, 2624], P(None, 'row', 'col'), may hold values from -1 to 8, as said below
Outputs:
- factored: float32 [328, 64, 8, 2624], P(None, 'row', 'col')
The draws below stay inside these ranges and needn't reach their ends.
Inputs may be any that keep to these rules, and one draw needn't show every extreme that they name: kernel is symmetric (entry i, j equals entry j, i), and its leading 2 * 256 rows and columns form a positive definite matrix.
All inputs are finite; a program needn't handle non-finite values.
Results may differ from the reference program's by a relative error of at most 0.0086.
Values may be sent and summed in bfloat16 or wider, within the bound.
No kernel may reach another device: no remote copies, remote signals or barrier semaphores. Data moves between devices by JAX's collectives and lax.ppermute only.
A program may use at most 64 MiB of HBM per device.

```python
import jax
import jax.numpy as jnp
from jax import lax

B = 256
STEPS = 2
N = 20992
N_ROW = 64
N_COL = 8


def draw_kernel(key, part):
    key_noise = jax.random.fold_in(key, 11)
    key_head = jax.random.fold_in(key, 12)
    key_tail = jax.random.fold_in(key, 13)
    noise = jnp.clip(jax.random.normal(key_noise, (N, N), jnp.float32), -4.0, 4.0)
    position = jnp.arange(N)
    head = position < STEPS * B
    both = jnp.logical_and(head[:, None], head[None, :])
    either = jnp.logical_or(head[:, None], head[None, :])
    scale = jnp.where(both, 0.065, jnp.where(either, 0.15, 0.04)).astype(jnp.float32)
    paired = (noise + noise.T) * 0.70710678 * scale
    diag_head = jax.random.uniform(key_head, (N,), jnp.float32, 3.0, 4.0)
    diag_tail = jax.random.uniform(key_tail, (N,), jnp.float32, 5.0, 8.0)
    diagonal = jnp.where(head, diag_head, diag_tail)
    full = jnp.where(position[:, None] == position[None, :], diagonal[:, None], paired)
    return jnp.transpose(full.reshape(N // N_ROW, N_ROW, N // N_COL, N_COL), (0, 1, 3, 2)).astype(jnp.bfloat16)


def setup_inputs(seed: int = 0) -> dict:
    seeds = jax.random.split(jax.random.key(seed), 2)
    return {
        "kernel": draw_kernel(jax.random.fold_in(seeds[1], 71), 0),
    }


def reference(kernel):
    full = jnp.transpose(kernel, (0, 1, 3, 2)).reshape(N, N).astype(jnp.float32)
    eye = jnp.eye(B, dtype=jnp.float32)
    for step in range(STEPS):
        low = step * B
        high = low + B
        rest = N - high
        corner = full[low:high, low:high]
        factor = jnp.linalg.cholesky(corner)
        inverse = jax.scipy.linalg.solve_triangular(factor, eye, lower=True)
        inverse_b = inverse.astype(jnp.bfloat16)
        column_b = full[high:, low:high].astype(jnp.bfloat16)
        solved = lax.dot_general(column_b.astype(jnp.float32), inverse_b.astype(jnp.float32), (((1,), (1,)), ((), ())), preferred_element_type=jnp.float32)
        solved_b = solved.astype(jnp.bfloat16)

        def update_block(index, matrix):
            start = (high + index * B).astype(jnp.int32)
            rows_b = lax.dynamic_slice_in_dim(solved_b, (index * B).astype(jnp.int32), B, 0)
            product = lax.dot_general(rows_b.astype(jnp.float32), solved_b.astype(jnp.float32), (((1,), (1,)), ((), ())), preferred_element_type=jnp.float32)
            current = lax.dynamic_slice(matrix, (start, jnp.int32(high)), (B, rest))
            return lax.dynamic_update_slice(matrix, current - product, (start, jnp.int32(high)))
        full = lax.fori_loop(jnp.int32(0), jnp.int32(rest // B), update_block, full)
        full = full.at[low:high, low:high].set(factor)
        full = full.at[high:, low:high].set(solved)
        full = full.at[low:high, high:].set(solved.T)
    return jnp.transpose(full.reshape(N // N_ROW, N_ROW, N // N_COL, N_COL), (0, 1, 3, 2))
```

```python
import functools

import jax
import jax.numpy as jnp
import numpy as np
from jax import lax
from jax.experimental import pallas as pl
from jax.experimental.pallas import tpu as pltpu
from jax.sharding import Mesh, PartitionSpec as P

B = 256
STEPS = 2
T = STEPS * B
NB = 64
LANE = 128
NY, NZH, NZL, NX, NC = 4, 4, 4, 4, 2
ROWS, COLS = NY * NZH * NZL, NX * NC
LR, LC = T // ROWS, T // COLS
TILE = 384
HIGH = lax.Precision.HIGHEST
F32, BF16 = jnp.float32, jnp.bfloat16


def mm(a, b, ca=1, cb=0, precision=None):
    return lax.dot_general(
        a, b, (((ca,), (cb,)), ((), ())), precision=precision, preferred_element_type=F32
    )


def eliminate(block):
    row = lax.broadcasted_iota(jnp.int32, (NB, NB), 0)
    col = lax.broadcasted_iota(jnp.int32, (NB, NB), 1)
    eye = (row == col).astype(F32)
    full = jnp.concatenate([block, eye], axis=1)
    groups = NB // 8
    r = [full[8 * g : 8 * g + 8, :] for g in range(groups)]
    sub = lax.broadcasted_iota(jnp.int32, (8, 128), 0)
    scales = []
    for b in range(groups):
        c = [
            {g: jnp.broadcast_to(r[g][:, 8 * b + i : 8 * b + i + 1], (8, 128)) for g in range(b, groups)}
            for i in range(8)
        ]
        scale = jnp.zeros((8, 128), F32)
        for i in range(8):
            pivot = jnp.broadcast_to(c[i][b][i : i + 1, :], (8, 128))
            inv = 1.0 / pivot
            scale = jnp.where(sub == i, lax.rsqrt(pivot), scale)
            lead = jnp.broadcast_to(r[b][i : i + 1, :], (8, 128))
            ahead = {i2: jnp.broadcast_to(c[i2][b][i : i + 1, :], (8, 128)) for i2 in range(i + 1, 8)}
            for g in range(b, groups):
                m = c[i][g] * inv
                if g == b:
                    m = jnp.where(sub > i, m, 0.0)
                for i2 in range(i + 1, 8):
                    c[i2][g] = c[i2][g] - m * ahead[i2]
                r[g] = r[g] - m * lead
        scales.append(scale)
    out = jnp.concatenate([r[g] * scales[g] for g in range(groups)], axis=0)
    upper = jnp.where(row <= col, out[:, :NB], 0.0)
    lower = jnp.where(row >= col, out[:, NB:], 0.0)
    return upper, lower


def factor_panel(a):
    nb = B // NB
    cur = [[a[NB * i : NB * i + NB, NB * j : NB * j + NB] if i >= j else None for j in range(nb)] for i in range(nb)]
    up = [[None] * nb for _ in range(nb)]
    low = [[None] * nb for _ in range(nb)]
    inv = [[None] * nb for _ in range(nb)]
    zero = jnp.zeros((NB, NB), F32)
    for k in range(nb):
        u, g = eliminate(cur[k][k])
        up[k][k] = u
        inv[k][k] = g
        if k + 1 < nb:
            below = jnp.concatenate([cur[i][k] for i in range(k + 1, nb)], axis=0)
            solved = mm(below, g, 1, 1, HIGH)
            for i in range(k + 1, nb):
                low[i][k] = solved[NB * (i - k - 1) : NB * (i - k), :]
            upper = mm(g, below, 1, 1, HIGH)
            for i in range(k + 1, nb):
                up[k][i] = upper[:, NB * (i - k - 1) : NB * (i - k)]
            for j in range(k + 1, nb):
                prod = mm(solved[NB * (j - k - 1) :, :], low[j][k], 1, 1, HIGH)
                for i in range(j, nb):
                    cur[i][j] = cur[i][j] - prod[NB * (i - j) : NB * (i - j + 1), :]
        if k:
            left = jnp.concatenate(low[k][:k], axis=1)
            prev = jnp.concatenate(
                [jnp.concatenate([inv[i][j] if j <= i else zero for j in range(k)], axis=1) for i in range(k)], axis=0
            )
            row = -mm(g, mm(left, prev, 1, 0, HIGH), 1, 0, HIGH)
            for j in range(k):
                inv[k][j] = row[:, NB * j : NB * j + NB]
    upper = jnp.concatenate(
        [jnp.concatenate([up[i][j] if j >= i else zero for j in range(nb)], axis=1) for i in range(nb)], axis=0
    )
    inverse = jnp.concatenate(
        [jnp.concatenate([inv[i][j] if j <= i else zero for j in range(nb)], axis=1) for i in range(nb)], axis=0
    )
    return upper, inverse


def factor_kernel(pos_ref, x_ref, prow_ref, pcol_ref, head_ref, g_ref, l_ref, own_ref, u_scr, a_scr):
    acc = None
    for y in range(NY):
        flat = jnp.concatenate([x_ref[y, k] for k in range(COLS)], axis=1)
        part = mm(flat, pcol_ref[...]).astype(BF16)
        rows = NZH * NZL * LR
        term = mm(prow_ref[:, rows * y : rows * y + rows], part)
        acc = term if acc is None else acc + term
    a_scr[...] = acc
    u1, g1 = factor_panel(a_scr[0:B, 0:B])
    g1b = g1.astype(BF16)
    s21 = mm(a_scr[B:T, 0:B].astype(BF16), g1b, 1, 1)
    s12 = mm(g1b, a_scr[0:B, B:T].astype(BF16), 1, 0)
    s21b = s21.astype(BF16)
    a22 = a_scr[B:T, B:T] - mm(s21b, s21b, 1, 1)
    u2, g2 = factor_panel(a22)
    g2b = g2.astype(BF16)
    g_ref[0] = g1b
    g_ref[1] = g2b
    l_ref[...] = s21b
    head_ref[0:B, :] = mm(g1b, prow_ref[0:B, :]).astype(BF16)
    head_ref[B:T, :] = prow_ref[B:T, :]
    for k in range(B // LANE):
        lanes = slice(LANE * k, LANE * k + LANE)
        u_scr[k, 0:B, :] = u1.T[:, lanes]
        u_scr[k, B:T, :] = s21[:, lanes]
        u_scr[B // LANE + k, 0:B, :] = s12[:, lanes]
        u_scr[B // LANE + k, B:T, :] = u2.T[:, lanes]
    r = pos_ref[0]
    q = pos_ref[1]
    own = jnp.concatenate([u_scr[k, pl.ds(r, LR, stride=ROWS), :] for k in range(T // LANE)], axis=1)
    pick = (
        lax.broadcasted_iota(jnp.int32, (T, LC), 0) == lax.broadcasted_iota(jnp.int32, (T, LC), 1) * COLS + q
    ).astype(F32)
    own_ref[...] = mm(own, pick, 1, 0, HIGH)


def update_kernel(pos_ref, head_ref, g_ref, l_ref, own_ref, wr_ref, x_ref, w_ref, out_ref, srow, scol, u_scr):
    step = pl.program_id(0)
    l21 = l_ref[...]

    @pl.when(step == 0)
    def _():
        q = pos_ref[1]
        s1 = mm(wr_ref[:, 0:B], g_ref[0], 1, 1)
        s1b = s1.astype(BF16)
        c2 = (wr_ref[:, B:T].astype(F32) - mm(s1b, l21, 1, 1)).astype(BF16)
        s2 = mm(c2, g_ref[1], 1, 1)
        srow[:, 0:B] = s1b
        srow[:, B:T] = s2.astype(BF16)
        pick = (
            lax.broadcasted_iota(jnp.int32, (B, LC // 2), 0)
            == lax.broadcasted_iota(jnp.int32, (B, LC // 2), 1) * COLS + q
        ).astype(F32)
        scol[:, 0 : LC // 2] = mm(s1, pick, 1, 0, HIGH)
        scol[:, LC // 2 : LC] = mm(s2, pick, 1, 0, HIGH)

    both = mm(head_ref[...], x_ref[...])
    u1 = both[0:B, :]
    u1b = u1.astype(BF16)
    c2 = (both[B:T, :] - mm(l21, u1b)).astype(BF16)
    u2 = mm(g_ref[1], c2)
    for k in range(TILE // LANE):
        u_scr[k, 0:B, :] = u1[:, LANE * k : LANE * k + LANE]
        u_scr[k, B:T, :] = u2[:, LANE * k : LANE * k + LANE]
    ub = jnp.concatenate([u1b, u2.astype(BF16)], axis=0)
    out_ref[...] = w_ref[...].astype(F32) - mm(srow[...], ub)
    for k in range(TILE // LANE):
        out_ref[0:LR, LANE * k : LANE * k + LANE] = u_scr[k, pl.ds(pos_ref[0], LR, stride=ROWS), :]

    @pl.when(step == 0)
    def _():
        out_ref[:, 0:LC] = scol[...]
        out_ref[0:LR, 0:LC] = own_ref[...]


def permutations():
    nat = np.arange(T)
    prow = np.zeros((T, T), np.float32)
    stored = (nat % ROWS) * LR + nat // ROWS
    prow[nat, stored] = 1
    pcol = np.zeros((T, T), np.float32)
    pcol[(nat % COLS) * LC + nat // COLS, nat] = 1
    return prow.astype(jnp.bfloat16), pcol.astype(jnp.bfloat16)


def factor(pos, corner, prow, pcol):
    vmem = pl.BlockSpec(memory_space=pltpu.VMEM)
    return pl.pallas_call(
        factor_kernel,
        out_shape=(
            jax.ShapeDtypeStruct((T, T), BF16),
            jax.ShapeDtypeStruct((STEPS, B, B), BF16),
            jax.ShapeDtypeStruct((B, B), BF16),
            jax.ShapeDtypeStruct((LR, LC), F32),
        ),
        in_specs=[pl.BlockSpec(memory_space=pltpu.SMEM), vmem, vmem, vmem],
        out_specs=(vmem, vmem, vmem, vmem),
        scratch_shapes=[pltpu.VMEM((T // LANE, T, LANE), F32), pltpu.VMEM((T, T), F32)],
        name="factor",
    )(pos, corner, prow, pcol)


def update(pos, head, g, l21, own, wr, x, w):
    rows, cols = w.shape
    whole = lambda *shape: pl.BlockSpec(shape, lambda i: (0,) * len(shape))
    return pl.pallas_call(
        update_kernel,
        grid=(pl.cdiv(cols, TILE),),
        out_shape=jax.ShapeDtypeStruct((rows, cols), F32),
        in_specs=[
            pl.BlockSpec(memory_space=pltpu.SMEM),
            whole(T, T),
            whole(STEPS, B, B),
            whole(B, B),
            whole(LR, LC),
            whole(rows, T),
            pl.BlockSpec((T, TILE), lambda i: (0, i)),
            pl.BlockSpec((rows, TILE), lambda i: (0, i)),
        ],
        out_specs=pl.BlockSpec((rows, TILE), lambda i: (0, i)),
        scratch_shapes=[
            pltpu.VMEM((rows, T), BF16),
            pltpu.VMEM((rows, LC), F32),
            pltpu.VMEM((TILE // LANE, T, LANE), F32),
        ],
        name="update",
    )(pos, head, g, l21, own, wr, x, w)


def everyone(x, axis, count):
    return lax.all_to_all(jnp.broadcast_to(x[None], (count,) + x.shape), axis, 0, 0, tiled=True)


def on_device(kernel):
    work = kernel[:, 0, 0, :]
    rows, cols = work.shape
    r = lax.axis_index(("y", "zh", "zl"))
    q = lax.axis_index(("x", "c"))
    pos = jnp.stack([r, q]).astype(jnp.int32)
    prow, pcol = permutations()
    prow, pcol = jnp.asarray(prow), jnp.asarray(pcol)
    head_rows = work[0:LR, :]

    corner = everyone(head_rows[:, 0:LC], ("zh", "zl"), NZH * NZL)
    corner = everyone(corner.reshape(NZH * NZL * LR, LC), ("y", "x", "c"), NY * COLS)
    corner = corner.reshape(NY, COLS, NZH * NZL * LR, LC)

    wr = everyone(work[:, 0:LC], ("x", "c"), COLS)
    wr = mm(jnp.transpose(wr, (1, 0, 2)).reshape(rows, T), pcol).astype(BF16)

    x = lax.all_gather(head_rows, ("zh", "zl"), axis=0, tiled=False)
    x = lax.all_gather(x.reshape(NZH * NZL * LR, cols), "y", axis=0, tiled=False)
    x = x.reshape(T, cols)

    head, g, l21, own = factor(pos, corner, prow, pcol)
    out = update(pos, head, g, l21, own, wr, x, work)
    return out[:, None, None, :]


def solution(mesh):
    inner = Mesh(mesh.devices.reshape(NY, NZH, NZL, NX, NC), ("y", "zh", "zl", "x", "c"))
    spec = P(None, ("y", "zh", "zl"), ("x", "c"), None)
    return jax.shard_map(on_device, mesh=inner, in_specs=(spec,), out_specs=spec, check_vma=False)
```

```python
import functools

import jax
import jax.numpy as jnp
import numpy as np
from jax import lax
from jax.experimental import pallas as pl
from jax.experimental.pallas import tpu as pltpu
from jax.sharding import Mesh, PartitionSpec as P

B = 256
STEPS = 2
T = STEPS * B
NB = 64
LANE = 128
FAR, NEAR = (4, -4, 8), (1, -1, 2)
NY, NZH, NZL, NX, NC = 4, 4, 4, 4, 2
NZ = NZH * NZL
ROWS, COLS = NY * NZH * NZL, NX * NC
LR, LC = T // ROWS, T // COLS
TILE = 384
HIGH = lax.Precision.HIGHEST
F32, BF16 = jnp.float32, jnp.bfloat16


def mm(a, b, ca=1, cb=0, precision=None):
    return lax.dot_general(
        a, b, (((ca,), (cb,)), ((), ())), precision=precision, preferred_element_type=F32
    )


def eliminate(block):
    row = lax.broadcasted_iota(jnp.int32, (NB, NB), 0)
    col = lax.broadcasted_iota(jnp.int32, (NB, NB), 1)
    eye = (row == col).astype(F32)
    full = jnp.concatenate([block, eye], axis=1)
    groups = NB // 8
    r = [full[8 * g : 8 * g + 8, :] for g in range(groups)]
    sub = lax.broadcasted_iota(jnp.int32, (8, 128), 0)
    scales = []
    for b in range(groups):
        c = [
            {g: jnp.broadcast_to(r[g][:, 8 * b + i : 8 * b + i + 1], (8, 128)) for g in range(b, groups)}
            for i in range(8)
        ]
        scale = jnp.zeros((8, 128), F32)
        for i in range(8):
            pivot = jnp.broadcast_to(c[i][b][i : i + 1, :], (8, 128))
            inv = 1.0 / pivot
            scale = jnp.where(sub == i, lax.rsqrt(pivot), scale)
            lead = jnp.broadcast_to(r[b][i : i + 1, :], (8, 128))
            ahead = {i2: jnp.broadcast_to(c[i2][b][i : i + 1, :], (8, 128)) for i2 in range(i + 1, 8)}
            for g in range(b, groups):
                m = c[i][g] * inv
                if g == b:
                    m = jnp.where(sub > i, m, 0.0)
                for i2 in range(i + 1, 8):
                    c[i2][g] = c[i2][g] - m * ahead[i2]
                r[g] = r[g] - m * lead
        scales.append(scale)
    out = jnp.concatenate([r[g] * scales[g] for g in range(groups)], axis=0)
    upper = jnp.where(row <= col, out[:, :NB], 0.0)
    lower = jnp.where(row >= col, out[:, NB:], 0.0)
    return upper, lower


def factor_panel(a):
    nb = B // NB
    cur = [[a[NB * i : NB * i + NB, NB * j : NB * j + NB] if i >= j else None for j in range(nb)] for i in range(nb)]
    up = [[None] * nb for _ in range(nb)]
    low = [[None] * nb for _ in range(nb)]
    inv = [[None] * nb for _ in range(nb)]
    zero = jnp.zeros((NB, NB), F32)
    for k in range(nb):
        u, g = eliminate(cur[k][k])
        up[k][k] = u
        inv[k][k] = g
        if k + 1 < nb:
            below = jnp.concatenate([cur[i][k] for i in range(k + 1, nb)], axis=0)
            solved = mm(below, g, 1, 1, HIGH)
            for i in range(k + 1, nb):
                low[i][k] = solved[NB * (i - k - 1) : NB * (i - k), :]
            upper = mm(g, below, 1, 1, HIGH)
            for i in range(k + 1, nb):
                up[k][i] = upper[:, NB * (i - k - 1) : NB * (i - k)]
            for j in range(k + 1, nb):
                prod = mm(solved[NB * (j - k - 1) :, :], low[j][k], 1, 1, HIGH)
                for i in range(j, nb):
                    cur[i][j] = cur[i][j] - prod[NB * (i - j) : NB * (i - j + 1), :]
        if k:
            left = jnp.concatenate(low[k][:k], axis=1)
            prev = jnp.concatenate(
                [jnp.concatenate([inv[i][j] if j <= i else zero for j in range(k)], axis=1) for i in range(k)], axis=0
            )
            row = -mm(g, mm(left, prev, 1, 0, HIGH), 1, 0, HIGH)
            for j in range(k):
                inv[k][j] = row[:, NB * j : NB * j + NB]
    upper = jnp.concatenate(
        [jnp.concatenate([up[i][j] if j >= i else zero for j in range(nb)], axis=1) for i in range(nb)], axis=0
    )
    inverse = jnp.concatenate(
        [jnp.concatenate([inv[i][j] if j <= i else zero for j in range(nb)], axis=1) for i in range(nb)], axis=0
    )
    return upper, inverse


def natural_rows(r, absolute):
    stored = lax.broadcasted_iota(jnp.int32, (B, T), 1)

    def shift(place, table):
        code = lax.rem(stored // place, 4)
        out = jnp.zeros_like(code)
        for k, d in enumerate(table):
            out = jnp.where(code == k + 1, d, out)
        return out

    z = lax.rem(lax.rem(r, NZ) - shift(LR, FAR) - shift(4 * LR, NEAR) + 2 * NZ, NZ)
    y = stored // (NZ * LR)
    if not absolute:
        y = lax.rem(r // NZ - shift(NZ * LR, NEAR) + 2 * NY, NY)
    return lax.rem(stored, LR) * ROWS + y * NZ + z


def factor_kernel(pos_ref, x_ref, pcol_ref, head_ref, g_ref, l_ref, own_ref, u_scr, a_scr):
    r = pos_ref[0]
    q = pos_ref[1]
    rows = lax.broadcasted_iota(jnp.int32, (B, T), 0)
    order = natural_rows(r, True)
    prow = jnp.concatenate([(rows == order).astype(BF16), (rows + B == order).astype(BF16)], axis=0)
    flat = jnp.concatenate([x_ref[y] for y in range(NY)], axis=1)
    part = mm(pcol_ref[...], flat).astype(BF16)
    a_scr[...] = mm(part, prow, 1, 1)
    u1, g1 = factor_panel(a_scr[0:B, 0:B])
    g1b = g1.astype(BF16)
    s21 = mm(a_scr[B:T, 0:B].astype(BF16), g1b, 1, 1)
    s12 = mm(g1b, a_scr[0:B, B:T].astype(BF16), 1, 0)
    s21b = s21.astype(BF16)
    a22 = a_scr[B:T, B:T] - mm(s21b, s21b, 1, 1)
    u2, g2 = factor_panel(a22)
    g2b = g2.astype(BF16)
    g_ref[0] = g1b
    g_ref[1] = g2b
    l_ref[...] = s21b
    order = natural_rows(r, False)
    head_ref[0:B, :] = mm(g1b, (rows == order).astype(BF16)).astype(BF16)
    head_ref[B:T, :] = (rows + B == order).astype(BF16)
    for k in range(B // LANE):
        lanes = slice(LANE * k, LANE * k + LANE)
        u_scr[k, 0:B, :] = u1.T[:, lanes]
        u_scr[k, B:T, :] = s21[:, lanes]
        u_scr[B // LANE + k, 0:B, :] = s12[:, lanes]
        u_scr[B // LANE + k, B:T, :] = u2.T[:, lanes]
    own = jnp.concatenate([u_scr[k, pl.ds(r, LR, stride=ROWS), :] for k in range(T // LANE)], axis=1)
    pick = (
        lax.broadcasted_iota(jnp.int32, (T, LC), 0) == lax.broadcasted_iota(jnp.int32, (T, LC), 1) * COLS + q
    ).astype(F32)
    own_ref[...] = mm(own, pick, 1, 0, HIGH)


def update_kernel(pos_ref, head_ref, g_ref, l_ref, own_ref, wr_ref, x0_ref, x1_ref, x2_ref, x3_ref, w_ref, out_ref, srow, scol, u_scr):
    step = pl.program_id(0)
    l21 = l_ref[...]

    @pl.when(step == 0)
    def _():
        q = pos_ref[1]
        s1 = mm(wr_ref[:, 0:B], g_ref[0], 1, 1)
        s1b = s1.astype(BF16)
        c2 = (wr_ref[:, B:T].astype(F32) - mm(s1b, l21, 1, 1)).astype(BF16)
        s2 = mm(c2, g_ref[1], 1, 1)
        srow[:, 0:B] = s1b
        srow[:, B:T] = s2.astype(BF16)
        pick = (
            lax.broadcasted_iota(jnp.int32, (B, LC // 2), 0)
            == lax.broadcasted_iota(jnp.int32, (B, LC // 2), 1) * COLS + q
        ).astype(F32)
        scol[:, 0 : LC // 2] = mm(s1, pick, 1, 0, HIGH)
        scol[:, LC // 2 : LC] = mm(s2, pick, 1, 0, HIGH)

    x = jnp.concatenate([ref[...] for ref in (x0_ref, x1_ref, x2_ref, x3_ref)], axis=0)
    both = mm(head_ref[...], x)
    u1 = both[0:B, :]
    u1b = u1.astype(BF16)
    c2 = (both[B:T, :] - mm(l21, u1b)).astype(BF16)
    u2 = mm(g_ref[1], c2)
    for k in range(TILE // LANE):
        u_scr[k, 0:B, :] = u1[:, LANE * k : LANE * k + LANE]
        u_scr[k, B:T, :] = u2[:, LANE * k : LANE * k + LANE]
    ub = jnp.concatenate([u1b, u2.astype(BF16)], axis=0)
    out_ref[:, 0, 0, :] = w_ref[...].astype(F32) - mm(srow[...], ub)
    for k in range(TILE // LANE):
        out_ref[0:LR, 0, 0, LANE * k : LANE * k + LANE] = u_scr[k, pl.ds(pos_ref[0], LR, stride=ROWS), :]

    @pl.when(step == 0)
    def _():
        out_ref[:, 0, 0, 0:LC] = scol[...]
        out_ref[0:LR, 0, 0, 0:LC] = own_ref[...]


def column_order():
    nat = np.arange(T)
    pcol = np.zeros((T, T), np.float32)
    pcol[nat, (nat % COLS) * LC + nat // COLS] = 1
    return pcol.astype(jnp.bfloat16)


def factor(pos, corner, pcol):
    vmem = pl.BlockSpec(memory_space=pltpu.VMEM)
    return pl.pallas_call(
        factor_kernel,
        out_shape=(
            jax.ShapeDtypeStruct((T, T), BF16),
            jax.ShapeDtypeStruct((STEPS, B, B), BF16),
            jax.ShapeDtypeStruct((B, B), BF16),
            jax.ShapeDtypeStruct((LR, LC), F32),
        ),
        in_specs=[pl.BlockSpec(memory_space=pltpu.SMEM), vmem, vmem],
        out_specs=(vmem, vmem, vmem, vmem),
        scratch_shapes=[pltpu.VMEM((T // LANE, T, LANE), F32), pltpu.VMEM((T, T), F32)],
        name="factor",
    )(pos, corner, pcol)


def update(pos, head, g, l21, own, wr, xs, w):
    rows, cols = w.shape
    whole = lambda *shape: pl.BlockSpec(shape, lambda i: (0,) * len(shape))
    return pl.pallas_call(
        update_kernel,
        grid=(pl.cdiv(cols, TILE),),
        out_shape=jax.ShapeDtypeStruct((rows, 1, 1, cols), F32),
        in_specs=[
            pl.BlockSpec(memory_space=pltpu.SMEM),
            whole(T, T),
            whole(STEPS, B, B),
            whole(B, B),
            whole(LR, LC),
            whole(rows, T),
            *[pl.BlockSpec((T // NY, TILE), lambda i: (0, i))] * NY,
            pl.BlockSpec((rows, TILE), lambda i: (0, i)),
        ],
        out_specs=pl.BlockSpec((rows, 1, 1, TILE), lambda i: (0, 0, 0, i)),
        scratch_shapes=[
            pltpu.VMEM((rows, T), BF16),
            pltpu.VMEM((rows, LC), F32),
            pltpu.VMEM((TILE // LANE, T, LANE), F32),
        ],
        name="update",
    )(pos, head, g, l21, own, wr, *xs, w)


def everyone(x, axis, count):
    return lax.all_to_all(jnp.broadcast_to(x[None], (count,) + x.shape), axis, 0, 0, tiled=True)


def spread(x, axis, count, shifts):
    parts = [lax.ppermute(x, axis, [(i, (i + d) % count) for i in range(count)]) for d in shifts]
    return [x] + parts


def on_device(kernel):
    work = kernel[:, 0, 0, :]
    rows, cols = work.shape
    r = lax.axis_index(("y", "zh", "zl"))
    q = lax.axis_index(("x", "c"))
    pos = jnp.stack([r, q]).astype(jnp.int32)
    pcol = jnp.asarray(column_order())
    head_rows = jnp.pad(work[0:LR, :], ((0, 0), (0, -cols % LANE)))

    x = jnp.concatenate(spread(head_rows, ("zh", "zl"), NZ, FAR), axis=0)
    x = jnp.concatenate(spread(x, ("zh", "zl"), NZ, NEAR), axis=0)
    corner = everyone(jnp.transpose(x[:, 0:LC]), ("y", "x", "c"), NY * COLS)
    corner = corner.reshape(NY, T, NZ * LR)
    xs = spread(x, "y", NY, NEAR)

    mine, corner = lax.optimization_barrier((work[:, 0:LC], corner))
    wr = everyone(jnp.transpose(mine), ("x", "c"), COLS).reshape(T, rows)
    wr = mm(wr, pcol, 0, 1).astype(BF16)

    head, g, l21, own = factor(pos, corner, pcol)
    return update(pos, head, g, l21, own, wr, xs, work)


def solution(mesh):
    inner = Mesh(mesh.devices.reshape(NY, NZH, NZL, NX, NC), ("y", "zh", "zl", "x", "c"))
    spec = P(None, ("y", "zh", "zl"), ("x", "c"), None)
    return jax.shard_map(on_device, mesh=inner, in_specs=(spec,), out_specs=spec, check_vma=False)
```

```python
import functools

import jax
import jax.numpy as jnp
import numpy as np
from jax import lax
from jax.experimental import pallas as pl
from jax.experimental.pallas import tpu as pltpu
from jax.sharding import Mesh, PartitionSpec as P

B = 256
STEPS = 2
T = STEPS * B
NB = 64
LANE = 128
WIDE = 16
FAR, NEAR = (4, -4, 8), (1, -1, 2)
NY, NZH, NZL, NX, NC = 4, 4, 4, 4, 2
NZ = NZH * NZL
ROWS, COLS = NY * NZH * NZL, NX * NC
LR, LC = T // ROWS, T // COLS
TILE = 896
HIGH = lax.Precision.HIGHEST
F32, BF16 = jnp.float32, jnp.bfloat16


def mm(a, b, ca=1, cb=0, precision=None):
    return lax.dot_general(
        a, b, (((ca,), (cb,)), ((), ())), precision=precision, preferred_element_type=F32
    )


def eliminate(block):
    row = lax.broadcasted_iota(jnp.int32, (NB, NB), 0)
    col = lax.broadcasted_iota(jnp.int32, (NB, NB), 1)
    eye = (row == col).astype(F32)
    full = jnp.concatenate([block, eye], axis=1)
    groups = NB // 8
    r = [full[8 * g : 8 * g + 8, :] for g in range(groups)]
    sub = lax.broadcasted_iota(jnp.int32, (8, 128), 0)
    scales = [jnp.zeros((8, 128), F32)] * groups
    for b in range(0, NB, WIDE):
        c = [
            {g: jnp.broadcast_to(r[g][:, b + i : b + i + 1], (8, 128)) for g in range(b // 8, groups)}
            for i in range(WIDE)
        ]
        for i in range(0, WIDE, 2):
            top, s = (b + i) // 8, (b + i) % 8
            line = lambda v, k: jnp.broadcast_to(v[k : k + 1, :], (8, 128))
            p, o, q = line(c[i][top], s), line(c[i + 1][top], s), line(c[i + 1][top], s + 1)
            det = p * q - o * o
            inv_p, inv_det = 1.0 / p, 1.0 / det
            tie = o * inv_p
            scales[top] = jnp.where(sub == s, lax.rsqrt(p), jnp.where(sub == s + 1, lax.rsqrt(det * inv_p), scales[top]))
            pd, od, qd = p * inv_det, o * inv_det, q * inv_det
            ahead = {k: (line(c[k][top], s), line(c[k][top], s + 1)) for k in range(i + 2, WIDE)}
            lead = (line(r[top], s), line(r[top], s + 1))
            for g in range(top, groups):
                m1 = c[i][g] * qd - c[i + 1][g] * od
                m2 = c[i + 1][g] * pd - c[i][g] * od
                if g == top:
                    m1 = jnp.where(sub > s + 1, m1, jnp.where(sub == s + 1, tie, 0.0))
                    m2 = jnp.where(sub > s + 1, m2, 0.0)
                for k in range(i + 2, WIDE):
                    c[k][g] = c[k][g] - (m1 * ahead[k][0] + m2 * ahead[k][1])
                r[g] = r[g] - (m1 * lead[0] + m2 * lead[1])
    out = jnp.concatenate([r[g] * scales[g] for g in range(groups)], axis=0)
    upper = jnp.where(row <= col, out[:, :NB], 0.0)
    lower = jnp.where(row >= col, out[:, NB:], 0.0)
    return upper, lower


def factor_panel(a):
    nb = B // NB
    cur = [[a[NB * i : NB * i + NB, NB * j : NB * j + NB] if i >= j else None for j in range(nb)] for i in range(nb)]
    up = [[None] * nb for _ in range(nb)]
    low = [[None] * nb for _ in range(nb)]
    inv = [[None] * nb for _ in range(nb)]
    zero = jnp.zeros((NB, NB), F32)
    for k in range(nb):
        u, g = eliminate(cur[k][k])
        up[k][k] = u
        inv[k][k] = g
        if k + 1 < nb:
            below = jnp.concatenate([cur[i][k] for i in range(k + 1, nb)], axis=0)
            solved = mm(below, g, 1, 1, HIGH)
            for i in range(k + 1, nb):
                low[i][k] = solved[NB * (i - k - 1) : NB * (i - k), :]
            upper = mm(g, below, 1, 1, HIGH)
            for i in range(k + 1, nb):
                up[k][i] = upper[:, NB * (i - k - 1) : NB * (i - k)]
            for j in range(k + 1, nb):
                prod = mm(solved[NB * (j - k - 1) :, :], low[j][k], 1, 1, HIGH)
                for i in range(j, nb):
                    cur[i][j] = cur[i][j] - prod[NB * (i - j) : NB * (i - j + 1), :]
        if k:
            left = jnp.concatenate(low[k][:k], axis=1)
            prev = jnp.concatenate(
                [jnp.concatenate([inv[i][j] if j <= i else zero for j in range(k)], axis=1) for i in range(k)], axis=0
            )
            row = -mm(g, mm(left, prev, 1, 0, HIGH), 1, 0, HIGH)
            for j in range(k):
                inv[k][j] = row[:, NB * j : NB * j + NB]
    upper = jnp.concatenate(
        [jnp.concatenate([up[i][j] if j >= i else zero for j in range(nb)], axis=1) for i in range(nb)], axis=0
    )
    inverse = jnp.concatenate(
        [jnp.concatenate([inv[i][j] if j <= i else zero for j in range(nb)], axis=1) for i in range(nb)], axis=0
    )
    return upper, inverse


def natural_rows(r, absolute):
    stored = lax.broadcasted_iota(jnp.int32, (8, T), 1)

    def shift(place, table):
        code = lax.rem(stored // place, 4)
        out = jnp.zeros_like(code)
        for k, d in enumerate(table):
            out = jnp.where(code == k + 1, d, out)
        return out

    z = lax.rem(lax.rem(r, NZ) - shift(LR, FAR) - shift(4 * LR, NEAR) + 2 * NZ, NZ)
    y = stored // (NZ * LR)
    if not absolute:
        y = lax.rem(r // NZ - shift(NZ * LR, NEAR) + 2 * NY, NY)
    order = lax.rem(stored, LR) * ROWS + y * NZ + z
    return jnp.broadcast_to(order[0:1, :], (B, T))


def factor_kernel(r_ref, q_ref, x_ref, pcol_ref, head_ref, side_ref, g_ref, l_ref, own_ref, u_scr, a_scr):
    r = r_ref[0]
    q = q_ref[0]
    rows = lax.broadcasted_iota(jnp.int32, (B, T), 0)
    order = natural_rows(r, True)
    prow = jnp.concatenate([(rows == order).astype(BF16), (rows + B == order).astype(BF16)], axis=0)
    flat = jnp.concatenate([x_ref[y] for y in range(NY)], axis=1)
    part = mm(pcol_ref[...], flat).astype(BF16)
    a_scr[...] = mm(part, prow, 1, 1)
    order = natural_rows(r, False)
    head_ref[B:T, :] = (rows + B == order).astype(BF16)
    side_ref[B:T, :] = pcol_ref[B:T, :]
    u1, g1 = factor_panel(a_scr[0:B, 0:B])
    g1b = g1.astype(BF16)
    s21 = mm(a_scr[B:T, 0:B].astype(BF16), g1b, 1, 1)
    s21b = s21.astype(BF16)
    a22 = a_scr[B:T, B:T] - mm(s21b, s21b, 1, 1)
    s12 = mm(g1b, a_scr[0:B, B:T].astype(BF16), 1, 0)
    l_ref[...] = s21b
    head_ref[0:B, :] = mm(g1b, (rows == order).astype(BF16)).astype(BF16)
    side_ref[0:B, :] = mm(g1b, pcol_ref[0:B, :]).astype(BF16)
    for k in range(B // LANE):
        lanes = slice(LANE * k, LANE * k + LANE)
        u_scr[k, 0:B, :] = u1.T[:, lanes]
        u_scr[k, B:T, :] = s21[:, lanes]
        u_scr[B // LANE + k, 0:B, :] = s12[:, lanes]
    pick = (
        lax.broadcasted_iota(jnp.int32, (T, LC), 0) == lax.broadcasted_iota(jnp.int32, (T, LC), 1) * COLS + q
    ).astype(F32)
    u2, g2 = factor_panel(a22)
    g_ref[...] = g2.astype(BF16)
    for k in range(B // LANE):
        u_scr[B // LANE + k, B:T, :] = u2.T[:, LANE * k : LANE * k + LANE]
    own = jnp.concatenate([u_scr[k, pl.ds(r, LR, stride=ROWS), :] for k in range(T // LANE)], axis=1)
    own_ref[...] = mm(own, pick, 1, 0, HIGH)


def update_kernel(
    r_ref, q_ref, head_ref, side_ref, g_ref, l_ref, own_ref, wr_ref, x0_ref, x1_ref, x2_ref, x3_ref, w_ref, out_ref,
    x_scr, w_scr, out_scr, s_scr, u_scr, x_sem, w_sem, out_sem,
):
    rows, cols = w_ref.shape
    spans = [(lo, min(TILE, cols - lo)) for lo in range(0, cols, TILE)]
    pieces = (x0_ref, x1_ref, x2_ref, x3_ref)
    x_copies = [
        [
            pltpu.make_async_copy(
                ref.at[:, pl.ds(lo, TILE)], x_scr.at[n, pl.ds(T // NY * k, T // NY), :], x_sem.at[n, k]
            )
            for k, ref in enumerate(pieces)
        ]
        for n, (lo, _) in enumerate(spans)
    ]
    w_copy = pltpu.make_async_copy(w_ref, w_scr, w_sem)
    for copy in x_copies[0]:
        copy.start()
    w_copy.start()
    for copies in x_copies[1:]:
        for copy in copies:
            copy.start()

    r, q = r_ref[0], q_ref[0]
    l21 = l_ref[...]
    g2 = g_ref[...]

    def solve(head, panel):
        both = mm(head, panel)
        u1 = both[0:B, :]
        u1b = u1.astype(BF16)
        c2 = (both[B:T, :] - mm(l21, u1b)).astype(BF16)
        u2 = mm(g2, c2)
        return u1, u2, jnp.concatenate([u1b, u2.astype(BF16)], axis=0)

    s1, s2, sb = solve(side_ref[...], wr_ref[...])
    srow = sb.T
    width = pl.cdiv(rows, LANE)
    for k in range(width):
        lanes = min(LANE, rows - LANE * k)
        s_scr[k, 0:B, 0:lanes] = s1[:, LANE * k : LANE * k + lanes]
        s_scr[k, B:T, 0:lanes] = s2[:, LANE * k : LANE * k + lanes]
    mine = jnp.concatenate([s_scr[k, pl.ds(q, LC, stride=COLS), :] for k in range(width)], axis=1)
    scol = mine.T[0:rows, :]

    out_copies = []
    for n, (lo, size) in enumerate(spans):
        for copy in x_copies[n]:
            copy.wait()
        u1, u2, ub = solve(head_ref[...], x_scr[n])
        for k in range(TILE // LANE):
            u_scr[k, 0:B, :] = u1[:, LANE * k : LANE * k + LANE]
            u_scr[k, B:T, :] = u2[:, LANE * k : LANE * k + LANE]
        if n == 0:
            w_copy.wait()
        done = mm(srow, ub)[:, 0:size]
        out_scr[:, 0, 0, lo : lo + size] = w_scr[:, lo : lo + size].astype(F32) - done
        for k in range(TILE // LANE):
            lanes = min(LANE, size - LANE * k)
            line = u_scr[k, pl.ds(r, LR, stride=ROWS), :]
            out_scr[0:LR, 0, 0, lo + LANE * k : lo + LANE * k + lanes] = line[:, 0:lanes]
        if n == 0:
            out_scr[:, 0, 0, 0:LC] = scol
            out_scr[0:LR, 0, 0, 0:LC] = own_ref[...]
        copy = pltpu.make_async_copy(
            out_scr.at[:, :, :, pl.ds(lo, size)], out_ref.at[:, :, :, pl.ds(lo, size)], out_sem.at[n]
        )
        copy.start()
        out_copies.append(copy)
    for copy in out_copies:
        copy.wait()


def column_order():
    nat = np.arange(T)
    pcol = np.zeros((T, T), np.float32)
    pcol[nat, (nat % COLS) * LC + nat // COLS] = 1
    return pcol.astype(jnp.bfloat16)


def factor(pos, corner, pcol):
    vmem = pl.BlockSpec(memory_space=pltpu.VMEM)
    return pl.pallas_call(
        factor_kernel,
        out_shape=(
            jax.ShapeDtypeStruct((T, T), BF16),
            jax.ShapeDtypeStruct((T, T), BF16),
            jax.ShapeDtypeStruct((B, B), BF16),
            jax.ShapeDtypeStruct((B, B), BF16),
            jax.ShapeDtypeStruct((LR, LC), F32),
        ),
        in_specs=[pl.BlockSpec(memory_space=pltpu.SMEM)] * 2 + [vmem] * 2,
        out_specs=(vmem,) * 5,
        scratch_shapes=[pltpu.VMEM((T // LANE, T, LANE), F32), pltpu.VMEM((T, T), F32)],
        cost_estimate=pl.CostEstimate(flops=40_000_000_000, transcendentals=0, bytes_accessed=4 * T * T),
        name="factor",
    )(*pos, corner, pcol)


def update(pos, head, side, g2, l21, own, wr, xs, w):
    rows, cols = w.shape
    steps = pl.cdiv(cols, TILE)
    whole = lambda a: pl.BlockSpec(a.shape, lambda i: (0,) * a.ndim)
    hbm = pl.BlockSpec(memory_space=pl.ANY)
    return pl.pallas_call(
        update_kernel,
        grid=(1,),
        out_shape=jax.ShapeDtypeStruct((rows, 1, 1, cols), F32),
        in_specs=[pl.BlockSpec(memory_space=pltpu.SMEM)] * 2
        + [whole(a) for a in (head, side, g2, l21, own, wr)]
        + [hbm] * (NY + 1),
        out_specs=hbm,
        scratch_shapes=[
            pltpu.VMEM((steps, T, TILE), BF16),
            pltpu.VMEM((rows, cols), BF16),
            pltpu.VMEM((rows, 1, 1, cols), F32),
            pltpu.VMEM((pl.cdiv(rows, LANE), T, LANE), F32),
            pltpu.VMEM((TILE // LANE, T, LANE), F32),
            pltpu.SemaphoreType.DMA((steps, NY)),
            pltpu.SemaphoreType.DMA,
            pltpu.SemaphoreType.DMA((steps,)),
        ],
        name="update",
    )(*pos, head, side, g2, l21, own, wr, *xs, w)


def everyone(x, axis, count):
    return lax.all_to_all(jnp.broadcast_to(x[None], (count,) + x.shape), axis, 0, 0, tiled=True)


def spread(x, axis, count, shifts):
    parts = [lax.ppermute(x, axis, [(i, (i + d) % count) for i in range(count)]) for d in shifts]
    return [x] + parts


def on_device(kernel):
    work = kernel[:, 0, 0, :]
    rows, cols = work.shape
    r = lax.axis_index(("y", "zh", "zl"))
    q = lax.axis_index(("x", "c"))
    pos = (r.reshape(1).astype(jnp.int32), q.reshape(1).astype(jnp.int32))
    pcol = jnp.asarray(column_order())
    head_rows = jnp.pad(work[0:LR, :], ((0, 0), (0, -cols % LANE)))

    wr = everyone(jnp.transpose(work[:, 0:LC]), ("x", "c"), COLS).reshape(T, rows)

    x = jnp.concatenate(spread(head_rows, ("zh", "zl"), NZ, FAR), axis=0)
    x = jnp.concatenate(spread(x, ("zh", "zl"), NZ, NEAR), axis=0)
    x, wr = lax.optimization_barrier((x, wr))
    pieces = jnp.broadcast_to(jnp.transpose(x[:, 0:LC])[None], (NY * COLS, LC, NZ * LR))
    x, pieces = lax.optimization_barrier((x, pieces))
    corner = lax.all_to_all(pieces, ("y", "x", "c"), 0, 0, tiled=True).reshape(NY, T, NZ * LR)
    xs = spread(x, "y", NY, NEAR)

    head, side, g2, l21, own = factor(pos, corner, pcol)
    return update(pos, head, side, g2, l21, own, wr, xs, work)


def solution(mesh):
    inner = Mesh(mesh.devices.reshape(NY, NZH, NZL, NX, NC), ("y", "zh", "zl", "x", "c"))
    spec = P(None, ("y", "zh", "zl"), ("x", "c"), None)
    return jax.shard_map(on_device, mesh=inner, in_specs=(spec,), out_specs=spec, check_vma=False)
```

```python
import functools

import jax
import jax.numpy as jnp
import numpy as np
from jax import lax
from jax.experimental import pallas as pl
from jax.experimental.pallas import tpu as pltpu
from jax.sharding import Mesh, PartitionSpec as P

B = 256
STEPS = 2
T = STEPS * B
NB = 64
LANE = 128
WIDE = 16
FAR, NEAR = (4, -4, 8), (1, -1, 2)
NY, NZH, NZL, NX, NC = 4, 4, 4, 4, 2
NZ = NZH * NZL
ROWS, COLS = NY * NZH * NZL, NX * NC
LR, LC = T // ROWS, T // COLS
TILE = 896
HIGH = lax.Precision.HIGHEST
F32, BF16 = jnp.float32, jnp.bfloat16


def mm(a, b, ca=1, cb=0, precision=None):
    return lax.dot_general(
        a, b, (((ca,), (cb,)), ((), ())), precision=precision, preferred_element_type=F32
    )


def eliminate(block):
    row = lax.broadcasted_iota(jnp.int32, (NB, NB), 0)
    col = lax.broadcasted_iota(jnp.int32, (NB, NB), 1)
    eye = (row == col).astype(F32)
    full = jnp.concatenate([block, eye], axis=1)
    groups = NB // 8
    r = [full[8 * g : 8 * g + 8, :] for g in range(groups)]
    sub = lax.broadcasted_iota(jnp.int32, (8, 128), 0)
    scales = [jnp.zeros((8, 128), F32)] * groups
    for b in range(0, NB, WIDE):
        c = [
            {g: jnp.broadcast_to(r[g][:, b + i : b + i + 1], (8, 128)) for g in range(b // 8, groups)}
            for i in range(WIDE)
        ]
        for i in range(0, WIDE, 2):
            top, s = (b + i) // 8, (b + i) % 8
            line = lambda v, k: jnp.broadcast_to(v[k : k + 1, :], (8, 128))
            p, o, q = line(c[i][top], s), line(c[i + 1][top], s), line(c[i + 1][top], s + 1)
            det = p * q - o * o
            inv_p, inv_det = 1.0 / p, 1.0 / det
            tie = o * inv_p
            scales[top] = jnp.where(sub == s, lax.rsqrt(p), jnp.where(sub == s + 1, lax.rsqrt(det * inv_p), scales[top]))
            pd, od, qd = p * inv_det, o * inv_det, q * inv_det
            ahead = {k: (line(c[k][top], s), line(c[k][top], s + 1)) for k in range(i + 2, WIDE)}
            lead = (line(r[top], s), line(r[top], s + 1))
            for g in range(top, groups):
                m1 = c[i][g] * qd - c[i + 1][g] * od
                m2 = c[i + 1][g] * pd - c[i][g] * od
                if g == top:
                    m1 = jnp.where(sub > s + 1, m1, jnp.where(sub == s + 1, tie, 0.0))
                    m2 = jnp.where(sub > s + 1, m2, 0.0)
                for k in range(i + 2, WIDE):
                    c[k][g] = c[k][g] - (m1 * ahead[k][0] + m2 * ahead[k][1])
                r[g] = r[g] - (m1 * lead[0] + m2 * lead[1])
    out = jnp.concatenate([r[g] * scales[g] for g in range(groups)], axis=0)
    upper = jnp.where(row <= col, out[:, :NB], 0.0)
    lower = jnp.where(row >= col, out[:, NB:], 0.0)
    return upper, lower


def factor_panel(a):
    nb = B // NB
    cur = [[a[NB * i : NB * i + NB, NB * j : NB * j + NB] if i >= j else None for j in range(nb)] for i in range(nb)]
    up = [[None] * nb for _ in range(nb)]
    low = [[None] * nb for _ in range(nb)]
    inv = [[None] * nb for _ in range(nb)]
    zero = jnp.zeros((NB, NB), F32)
    for k in range(nb):
        u, g = eliminate(cur[k][k])
        up[k][k] = u
        inv[k][k] = g
        if k + 1 < nb:
            below = jnp.concatenate([cur[i][k] for i in range(k + 1, nb)], axis=0)
            solved = mm(below, g, 1, 1, HIGH)
            for i in range(k + 1, nb):
                low[i][k] = solved[NB * (i - k - 1) : NB * (i - k), :]
            upper = mm(g, below, 1, 1, HIGH)
            for i in range(k + 1, nb):
                up[k][i] = upper[:, NB * (i - k - 1) : NB * (i - k)]
            for j in range(k + 1, nb):
                prod = mm(solved[NB * (j - k - 1) :, :], low[j][k], 1, 1, HIGH)
                for i in range(j, nb):
                    cur[i][j] = cur[i][j] - prod[NB * (i - j) : NB * (i - j + 1), :]
        if k:
            left = jnp.concatenate(low[k][:k], axis=1)
            prev = jnp.concatenate(
                [jnp.concatenate([inv[i][j] if j <= i else zero for j in range(k)], axis=1) for i in range(k)], axis=0
            )
            row = -mm(g, mm(left, prev, 1, 0, HIGH), 1, 0, HIGH)
            for j in range(k):
                inv[k][j] = row[:, NB * j : NB * j + NB]
    upper = jnp.concatenate(
        [jnp.concatenate([up[i][j] if j >= i else zero for j in range(nb)], axis=1) for i in range(nb)], axis=0
    )
    inverse = jnp.concatenate(
        [jnp.concatenate([inv[i][j] if j <= i else zero for j in range(nb)], axis=1) for i in range(nb)], axis=0
    )
    return upper, inverse


def natural_rows(r, absolute):
    stored = lax.broadcasted_iota(jnp.int32, (8, T), 1)

    def shift(place, table):
        code = lax.rem(stored // place, 4)
        out = jnp.zeros_like(code)
        for k, d in enumerate(table):
            out = jnp.where(code == k + 1, d, out)
        return out

    z = lax.rem(lax.rem(r, NZ) - shift(LR, FAR) - shift(4 * LR, NEAR) + 2 * NZ, NZ)
    y = stored // (NZ * LR)
    if not absolute:
        y = lax.rem(r // NZ - shift(NZ * LR, NEAR) + 2 * NY, NY)
    order = lax.rem(stored, LR) * ROWS + y * NZ + z
    return jnp.broadcast_to(order[0:1, :], (B, T))


def factor_kernel(r_ref, q_ref, x_ref, pcol_ref, head_ref, side_ref, g_ref, l_ref, own_ref, u_scr, a_scr):
    r = r_ref[0]
    q = q_ref[0]
    rows = lax.broadcasted_iota(jnp.int32, (B, T), 0)
    order = natural_rows(r, True)
    prow = jnp.concatenate([(rows == order).astype(BF16), (rows + B == order).astype(BF16)], axis=0)
    flat = jnp.concatenate([x_ref[y] for y in range(NY)], axis=1)
    part = mm(pcol_ref[...], flat).astype(BF16)
    a_scr[...] = mm(part, prow, 1, 1)
    order = natural_rows(r, False)
    head_ref[B:T, :] = (rows + B == order).astype(BF16)
    side_ref[B:T, :] = pcol_ref[B:T, :]
    u1, g1 = factor_panel(a_scr[0:B, 0:B])
    g1b = g1.astype(BF16)
    s21 = mm(a_scr[B:T, 0:B].astype(BF16), g1b, 1, 1)
    s21b = s21.astype(BF16)
    a22 = a_scr[B:T, B:T] - mm(s21b, s21b, 1, 1)
    s12 = mm(g1b, a_scr[0:B, B:T].astype(BF16), 1, 0)
    l_ref[...] = s21b
    head_ref[0:B, :] = mm(g1b, (rows == order).astype(BF16)).astype(BF16)
    side_ref[0:B, :] = mm(g1b, pcol_ref[0:B, :]).astype(BF16)
    for k in range(B // LANE):
        lanes = slice(LANE * k, LANE * k + LANE)
        u_scr[k, 0:B, :] = u1.T[:, lanes]
        u_scr[k, B:T, :] = s21[:, lanes]
        u_scr[B // LANE + k, 0:B, :] = s12[:, lanes]
    pick = (
        lax.broadcasted_iota(jnp.int32, (T, LC), 0) == lax.broadcasted_iota(jnp.int32, (T, LC), 1) * COLS + q
    ).astype(F32)
    u2, g2 = factor_panel(a22)
    g_ref[...] = g2.astype(BF16)
    for k in range(B // LANE):
        u_scr[B // LANE + k, B:T, :] = u2.T[:, LANE * k : LANE * k + LANE]
    own = jnp.concatenate([u_scr[k, pl.ds(r, LR, stride=ROWS), :] for k in range(T // LANE)], axis=1)
    own_ref[...] = mm(own, pick, 1, 0, HIGH)


def update_kernel(
    r_ref, q_ref, head_ref, side_ref, g_ref, l_ref, own_ref, wr_ref,
    x0_ref, x1_ref, x2_ref, x3_ref, x4_ref, x5_ref, x6_ref, w_ref, out_ref,
    x_scr, w_scr, out_scr, s_scr, u_scr, x_sem, w_sem, out_sem,
):
    rows, cols = w_ref.shape
    spans = [(lo, min(TILE, cols - lo)) for lo in range(0, cols, TILE)]
    pieces = (x0_ref, x1_ref, x2_ref, x3_ref, x4_ref, x5_ref, x6_ref)
    starts = [sum(ref.shape[0] for ref in pieces[:k]) for k in range(len(pieces))]
    x_copies = [
        [
            pltpu.make_async_copy(
                ref.at[:, pl.ds(lo, TILE)], x_scr.at[n, pl.ds(starts[k], ref.shape[0]), :], x_sem.at[n, k]
            )
            for k, ref in enumerate(pieces)
        ]
        for n, (lo, _) in enumerate(spans)
    ]
    w_copy = pltpu.make_async_copy(w_ref, w_scr, w_sem)
    for copy in x_copies[0]:
        copy.start()
    w_copy.start()
    for copies in x_copies[1:]:
        for copy in copies:
            copy.start()

    r, q = r_ref[0], q_ref[0]
    l21 = l_ref[...]
    g2 = g_ref[...]

    def solve(head, panel):
        both = mm(head, panel)
        u1 = both[0:B, :]
        u1b = u1.astype(BF16)
        c2 = (both[B:T, :] - mm(l21, u1b)).astype(BF16)
        u2 = mm(g2, c2)
        return u1, u2, jnp.concatenate([u1b, u2.astype(BF16)], axis=0)

    s1, s2, sb = solve(side_ref[...], wr_ref[...])
    srow = sb.T
    width = pl.cdiv(rows, LANE)
    for k in range(width):
        lanes = min(LANE, rows - LANE * k)
        s_scr[k, 0:B, 0:lanes] = s1[:, LANE * k : LANE * k + lanes]
        s_scr[k, B:T, 0:lanes] = s2[:, LANE * k : LANE * k + lanes]
    mine = jnp.concatenate([s_scr[k, pl.ds(q, LC, stride=COLS), :] for k in range(width)], axis=1)
    scol = mine.T[0:rows, :]

    out_copies = []
    for n, (lo, size) in enumerate(spans):
        for copy in x_copies[n]:
            copy.wait()
        u1, u2, ub = solve(head_ref[...], x_scr[n])
        for k in range(TILE // LANE):
            u_scr[k, 0:B, :] = u1[:, LANE * k : LANE * k + LANE]
            u_scr[k, B:T, :] = u2[:, LANE * k : LANE * k + LANE]
        if n == 0:
            w_copy.wait()
        done = mm(srow, ub)[:, 0:size]
        out_scr[:, 0, 0, lo : lo + size] = w_scr[:, lo : lo + size].astype(F32) - done
        for k in range(TILE // LANE):
            lanes = min(LANE, size - LANE * k)
            line = u_scr[k, pl.ds(r, LR, stride=ROWS), :]
            out_scr[0:LR, 0, 0, lo + LANE * k : lo + LANE * k + lanes] = line[:, 0:lanes]
        if n == 0:
            out_scr[:, 0, 0, 0:LC] = scol
            out_scr[0:LR, 0, 0, 0:LC] = own_ref[...]
        copy = pltpu.make_async_copy(
            out_scr.at[:, :, :, pl.ds(lo, size)], out_ref.at[:, :, :, pl.ds(lo, size)], out_sem.at[n]
        )
        copy.start()
        out_copies.append(copy)
    for copy in out_copies:
        copy.wait()


def column_order():
    nat = np.arange(T)
    pcol = np.zeros((T, T), np.float32)
    pcol[nat, (nat % COLS) * LC + nat // COLS] = 1
    return pcol.astype(jnp.bfloat16)


def factor(pos, corner, pcol):
    vmem = pl.BlockSpec(memory_space=pltpu.VMEM)
    return pl.pallas_call(
        factor_kernel,
        out_shape=(
            jax.ShapeDtypeStruct((T, T), BF16),
            jax.ShapeDtypeStruct((T, T), BF16),
            jax.ShapeDtypeStruct((B, B), BF16),
            jax.ShapeDtypeStruct((B, B), BF16),
            jax.ShapeDtypeStruct((LR, LC), F32),
        ),
        in_specs=[pl.BlockSpec(memory_space=pltpu.SMEM)] * 2 + [vmem] * 2,
        out_specs=(vmem,) * 5,
        scratch_shapes=[pltpu.VMEM((T // LANE, T, LANE), F32), pltpu.VMEM((T, T), F32)],
        cost_estimate=pl.CostEstimate(flops=40_000_000_000, transcendentals=0, bytes_accessed=4 * T * T),
        compiler_params=pltpu.CompilerParams(vmem_limit_bytes=24 << 20),
        name="factor",
    )(*pos, corner, pcol)


def update(pos, head, side, g2, l21, own, wr, xs, w):
    rows, cols = w.shape
    steps = pl.cdiv(cols, TILE)
    whole = lambda a: pl.BlockSpec(a.shape, lambda i: (0,) * a.ndim)
    hbm = pl.BlockSpec(memory_space=pl.ANY)
    return pl.pallas_call(
        update_kernel,
        grid=(1,),
        out_shape=jax.ShapeDtypeStruct((rows, 1, 1, cols), F32),
        in_specs=[pl.BlockSpec(memory_space=pltpu.SMEM)] * 2
        + [whole(a) for a in (head, side, g2, l21, own, wr)]
        + [hbm] * (len(xs) + 1),
        out_specs=hbm,
        scratch_shapes=[
            pltpu.VMEM((steps, T, TILE), BF16),
            pltpu.VMEM((rows, cols), BF16),
            pltpu.VMEM((rows, 1, 1, cols), F32),
            pltpu.VMEM((pl.cdiv(rows, LANE), T, LANE), F32),
            pltpu.VMEM((TILE // LANE, T, LANE), F32),
            pltpu.SemaphoreType.DMA((steps, len(xs))),
            pltpu.SemaphoreType.DMA,
            pltpu.SemaphoreType.DMA((steps,)),
        ],
        compiler_params=pltpu.CompilerParams(vmem_limit_bytes=32 << 20),
        name="update",
    )(*pos, head, side, g2, l21, own, wr, *xs, w)


def everyone(x, axis, count):
    return lax.all_to_all(jnp.broadcast_to(x[None], (count,) + x.shape), axis, 0, 0, tiled=True)


def spread(x, axis, count, shifts):
    parts = [lax.ppermute(x, axis, [(i, (i + d) % count) for i in range(count)]) for d in shifts]
    return [x] + parts


def on_device(kernel):
    work = kernel[:, 0, 0, :]
    rows, cols = work.shape
    r = lax.axis_index(("y", "zh", "zl"))
    q = lax.axis_index(("x", "c"))
    pos = (r.reshape(1).astype(jnp.int32), q.reshape(1).astype(jnp.int32))
    pcol = jnp.asarray(column_order())
    head_rows = jnp.pad(work[0:LR, :], ((0, 0), (0, -cols % LANE)))

    wr = everyone(jnp.transpose(work[:, 0:LC]), ("x", "c"), COLS).reshape(T, rows)

    x = jnp.concatenate(spread(head_rows, ("zh", "zl"), NZ, FAR), axis=0)
    across = spread(x, "y", NY, NEAR[2:])[1]
    x = jnp.concatenate(spread(x, ("zh", "zl"), NZ, NEAR), axis=0)
    x, wr = lax.optimization_barrier((x, wr))
    pieces = jnp.broadcast_to(jnp.transpose(x[:, 0:LC])[None], (NY * COLS, LC, NZ * LR))
    x, across, pieces = lax.optimization_barrier((x, across, pieces))
    corner = lax.all_to_all(pieces, ("y", "x", "c"), 0, 0, tiled=True).reshape(NY, T, NZ * LR)
    xs = spread(x, "y", NY, NEAR[:2]) + spread(across, ("zh", "zl"), NZ, NEAR)

    head, side, g2, l21, own = factor(pos, corner, pcol)
    return update(pos, head, side, g2, l21, own, wr, xs, work)


def solution(mesh):
    inner = Mesh(mesh.devices.reshape(NY, NZH, NZL, NX, NC), ("y", "zh", "zl", "x", "c"))
    spec = P(None, ("y", "zh", "zl"), ("x", "c"), None)
    return jax.shard_map(on_device, mesh=inner, in_specs=(spec,), out_specs=spec, check_vma=False)
```

```python
import jax
import jax.numpy as jnp
from jax import lax
from jax.experimental import pallas as pl
from jax.experimental.pallas import tpu as pltpu
from jax.sharding import Mesh, PartitionSpec as P

B = 256
STEPS = 2
T = STEPS * B
NB = 64
LANE = 128
WIDE = 16
FAR, NEAR = (4, -4, 8), (1, -1, 2)
NY, NZH, NZL, NX, NC = 4, 4, 4, 4, 2
NZ = NZH * NZL
ROWS, COLS = NY * NZH * NZL, NX * NC
LR, LC = T // ROWS, T // COLS
TILE = 896
HIGH = lax.Precision.HIGHEST
F32, BF16 = jnp.float32, jnp.bfloat16


def mm(a, b, ca=1, cb=0, precision=None):
    return lax.dot_general(
        a, b, (((ca,), (cb,)), ((), ())), precision=precision, preferred_element_type=F32
    )


def eliminate(block):
    row = lax.broadcasted_iota(jnp.int32, (NB, NB), 0)
    col = lax.broadcasted_iota(jnp.int32, (NB, NB), 1)
    eye = (row == col).astype(F32)
    full = jnp.concatenate([block, eye], axis=1)
    groups = NB // 8
    r = [full[8 * g : 8 * g + 8, :] for g in range(groups)]
    sub = lax.broadcasted_iota(jnp.int32, (8, 128), 0)
    scales = [jnp.zeros((8, 128), F32)] * groups
    for b in range(0, NB, WIDE):
        c = [
            {g: jnp.broadcast_to(r[g][:, b + i : b + i + 1], (8, 128)) for g in range(b // 8, groups)}
            for i in range(WIDE)
        ]
        for i in range(0, WIDE, 2):
            top, s = (b + i) // 8, (b + i) % 8
            line = lambda v, k: jnp.broadcast_to(v[k : k + 1, :], (8, 128))
            p, o, q = line(c[i][top], s), line(c[i + 1][top], s), line(c[i + 1][top], s + 1)
            det = p * q - o * o
            inv_p, inv_det = 1.0 / p, 1.0 / det
            tie = o * inv_p
            scales[top] = jnp.where(sub == s, lax.rsqrt(p), jnp.where(sub == s + 1, lax.rsqrt(det * inv_p), scales[top]))
            pd, od, qd = p * inv_det, o * inv_det, q * inv_det
            ahead = {k: (line(c[k][top], s), line(c[k][top], s + 1)) for k in range(i + 2, WIDE)}
            lead = (line(r[top], s), line(r[top], s + 1))
            for g in range(top, groups):
                m1 = c[i][g] * qd - c[i + 1][g] * od
                m2 = c[i + 1][g] * pd - c[i][g] * od
                if g == top:
                    m1 = jnp.where(sub > s + 1, m1, jnp.where(sub == s + 1, tie, 0.0))
                    m2 = jnp.where(sub > s + 1, m2, 0.0)
                for k in range(i + 2, WIDE):
                    c[k][g] = c[k][g] - (m1 * ahead[k][0] + m2 * ahead[k][1])
                r[g] = r[g] - (m1 * lead[0] + m2 * lead[1])
    out = jnp.concatenate([r[g] * scales[g] for g in range(groups)], axis=0)
    upper = jnp.where(row <= col, out[:, :NB], 0.0)
    lower = jnp.where(row >= col, out[:, NB:], 0.0)
    return upper, lower


def factor_panel(a):
    nb = B // NB
    cur = [[a[NB * i : NB * i + NB, NB * j : NB * j + NB] if i >= j else None for j in range(nb)] for i in range(nb)]
    up = [[None] * nb for _ in range(nb)]
    low = [[None] * nb for _ in range(nb)]
    inv = [[None] * nb for _ in range(nb)]
    zero = jnp.zeros((NB, NB), F32)
    for k in range(nb):
        u, g = eliminate(cur[k][k])
        up[k][k] = u
        inv[k][k] = g
        if k + 1 < nb:
            below = jnp.concatenate([cur[i][k] for i in range(k + 1, nb)], axis=0)
            solved = mm(below, g, 1, 1, HIGH)
            for i in range(k + 1, nb):
                low[i][k] = solved[NB * (i - k - 1) : NB * (i - k), :]
            upper = mm(g, below, 1, 1, HIGH)
            for i in range(k + 1, nb):
                up[k][i] = upper[:, NB * (i - k - 1) : NB * (i - k)]
            for j in range(k + 1, nb):
                prod = mm(solved[NB * (j - k - 1) :, :], low[j][k], 1, 1, HIGH)
                for i in range(j, nb):
                    cur[i][j] = cur[i][j] - prod[NB * (i - j) : NB * (i - j + 1), :]
        if k:
            left = jnp.concatenate(low[k][:k], axis=1)
            prev = jnp.concatenate(
                [jnp.concatenate([inv[i][j] if j <= i else zero for j in range(k)], axis=1) for i in range(k)], axis=0
            )
            row = -mm(g, mm(left, prev, 1, 0, HIGH), 1, 0, HIGH)
            for j in range(k):
                inv[k][j] = row[:, NB * j : NB * j + NB]
    upper = jnp.concatenate(
        [jnp.concatenate([up[i][j] if j >= i else zero for j in range(nb)], axis=1) for i in range(nb)], axis=0
    )
    inverse = jnp.concatenate(
        [jnp.concatenate([inv[i][j] if j <= i else zero for j in range(nb)], axis=1) for i in range(nb)], axis=0
    )
    return upper, inverse


def natural_rows(r, absolute):
    stored = lax.broadcasted_iota(jnp.int32, (8, T), 1)

    def shift(place, table):
        code = lax.rem(stored // place, 4)
        out = jnp.zeros_like(code)
        for k, d in enumerate(table):
            out = jnp.where(code == k + 1, d, out)
        return out

    z = lax.rem(lax.rem(r, NZ) - shift(LR, FAR) - shift(4 * LR, NEAR) + 2 * NZ, NZ)
    y = stored // (NZ * LR)
    if not absolute:
        y = lax.rem(r // NZ - shift(NZ * LR, NEAR) + 2 * NY, NY)
    order = lax.rem(stored, LR) * ROWS + y * NZ + z
    return jnp.broadcast_to(order[0:1, :], (B, T))


def factor_kernel(r_ref, q_ref, x_ref, head_ref, side_ref, g_ref, l_ref, own_ref, u_scr, a_scr):
    r = r_ref[0]
    q = q_ref[0]
    rows = lax.broadcasted_iota(jnp.int32, (B, T), 0)
    order = natural_rows(r, True)
    prow = jnp.concatenate([(rows == order).astype(BF16), (rows + B == order).astype(BF16)], axis=0)
    flat = jnp.concatenate([x_ref[y] for y in range(NY)], axis=1)
    stored = lax.broadcasted_iota(jnp.int32, (8, T), 1)
    column = jnp.broadcast_to((lax.rem(stored, LC) * COLS + stored // LC)[0:1, :], (B, T))
    pcol = [(rows == column).astype(BF16), (rows + B == column).astype(BF16)]
    part = mm(jnp.concatenate(pcol, axis=0), flat).astype(BF16)
    a_scr[...] = mm(part, prow, 1, 1)
    order = natural_rows(r, False)
    head_ref[B:T, :] = (rows + B == order).astype(BF16)
    side_ref[B:T, :] = pcol[1]
    u1, g1 = factor_panel(a_scr[0:B, 0:B])
    g1b = g1.astype(BF16)
    s21 = mm(a_scr[B:T, 0:B].astype(BF16), g1b, 1, 1)
    s21b = s21.astype(BF16)
    a22 = a_scr[B:T, B:T] - mm(s21b, s21b, 1, 1)
    s12 = mm(g1b, a_scr[0:B, B:T].astype(BF16), 1, 0)
    l_ref[...] = s21b
    head_ref[0:B, :] = mm(g1b, (rows == order).astype(BF16)).astype(BF16)
    side_ref[0:B, :] = mm(g1b, pcol[0]).astype(BF16)
    for k in range(B // LANE):
        lanes = slice(LANE * k, LANE * k + LANE)
        u_scr[k, 0:B, :] = u1.T[:, lanes]
        u_scr[k, B:T, :] = s21[:, lanes]
        u_scr[B // LANE + k, 0:B, :] = s12[:, lanes]
    pick = (
        lax.broadcasted_iota(jnp.int32, (T, LC), 0) == lax.broadcasted_iota(jnp.int32, (T, LC), 1) * COLS + q
    ).astype(F32)
    u2, g2 = factor_panel(a22)
    g_ref[...] = g2.astype(BF16)
    for k in range(B // LANE):
        u_scr[B // LANE + k, B:T, :] = u2.T[:, LANE * k : LANE * k + LANE]
    own = jnp.concatenate([u_scr[k, pl.ds(r, LR, stride=ROWS), :] for k in range(T // LANE)], axis=1)
    own_ref[...] = mm(own, pick, 1, 0, HIGH)


def update_kernel(
    r_ref, q_ref, head_ref, side_ref, g_ref, l_ref, own_ref, wr_ref,
    x0_ref, x1_ref, x2_ref, x3_ref, x4_ref, x5_ref, x6_ref, w_ref, out_ref,
    x_scr, w_scr, out_scr, s_scr, u_scr, x_sem, w_sem, out_sem,
):
    rows, cols = w_ref.shape
    spans = [(lo, min(TILE, cols - lo)) for lo in range(0, cols, TILE)]
    pieces = (x0_ref, x1_ref, x2_ref, x3_ref, x4_ref, x5_ref, x6_ref)
    starts = [sum(ref.shape[0] for ref in pieces[:k]) for k in range(len(pieces))]
    x_copies = [
        [
            pltpu.make_async_copy(
                ref.at[:, pl.ds(lo, TILE)], x_scr.at[n, pl.ds(starts[k], ref.shape[0]), :], x_sem.at[n, k]
            )
            for k, ref in enumerate(pieces)
        ]
        for n, (lo, _) in enumerate(spans)
    ]
    w_copy = pltpu.make_async_copy(w_ref, w_scr, w_sem)
    for copy in x_copies[0]:
        copy.start()
    w_copy.start()
    for copies in x_copies[1:]:
        for copy in copies:
            copy.start()

    r, q = r_ref[0], q_ref[0]
    l21 = l_ref[...]
    g2 = g_ref[...]

    def solve(head, panel):
        both = mm(head, panel)
        u1 = both[0:B, :]
        u1b = u1.astype(BF16)
        c2 = (both[B:T, :] - mm(l21, u1b)).astype(BF16)
        u2 = mm(g2, c2)
        return u1, u2, jnp.concatenate([u1b, u2.astype(BF16)], axis=0)

    s1, s2, sb = solve(side_ref[...], wr_ref[...])
    srow = sb.T
    width = pl.cdiv(rows, LANE)
    for k in range(width):
        lanes = min(LANE, rows - LANE * k)
        s_scr[k, 0:B, 0:lanes] = s1[:, LANE * k : LANE * k + lanes]
        s_scr[k, B:T, 0:lanes] = s2[:, LANE * k : LANE * k + lanes]
    mine = jnp.concatenate([s_scr[k, pl.ds(q, LC, stride=COLS), :] for k in range(width)], axis=1)
    scol = mine.T[0:rows, :]

    out_copies = []
    for n, (lo, size) in enumerate(spans):
        for copy in x_copies[n]:
            copy.wait()
        u1, u2, ub = solve(head_ref[...], x_scr[n])
        for k in range(TILE // LANE):
            u_scr[k, 0:B, :] = u1[:, LANE * k : LANE * k + LANE]
            u_scr[k, B:T, :] = u2[:, LANE * k : LANE * k + LANE]
        if n == 0:
            w_copy.wait()
        done = mm(srow, ub)[:, 0:size]
        out_scr[:, 0, 0, lo : lo + size] = w_scr[:, lo : lo + size].astype(F32) - done
        for k in range(TILE // LANE):
            lanes = min(LANE, size - LANE * k)
            line = u_scr[k, pl.ds(r, LR, stride=ROWS), :]
            out_scr[0:LR, 0, 0, lo + LANE * k : lo + LANE * k + lanes] = line[:, 0:lanes]
        if n == 0:
            out_scr[:, 0, 0, 0:LC] = scol
            out_scr[0:LR, 0, 0, 0:LC] = own_ref[...]
        copy = pltpu.make_async_copy(
            out_scr.at[:, :, :, pl.ds(lo, size)], out_ref.at[:, :, :, pl.ds(lo, size)], out_sem.at[n]
        )
        copy.start()
        out_copies.append(copy)
    for copy in out_copies:
        copy.wait()


def factor(pos, corner):
    vmem = pl.BlockSpec(memory_space=pltpu.VMEM)
    return pl.pallas_call(
        factor_kernel,
        out_shape=(
            jax.ShapeDtypeStruct((T, T), BF16),
            jax.ShapeDtypeStruct((T, T), BF16),
            jax.ShapeDtypeStruct((B, B), BF16),
            jax.ShapeDtypeStruct((B, B), BF16),
            jax.ShapeDtypeStruct((LR, LC), F32),
        ),
        in_specs=[pl.BlockSpec(memory_space=pltpu.SMEM)] * 2 + [vmem],
        out_specs=(vmem,) * 5,
        scratch_shapes=[pltpu.VMEM((T // LANE, T, LANE), F32), pltpu.VMEM((T, T), F32)],
        cost_estimate=pl.CostEstimate(flops=40_000_000_000, transcendentals=0, bytes_accessed=4 * T * T),
        compiler_params=pltpu.CompilerParams(vmem_limit_bytes=24 << 20),
        name="factor",
    )(*pos, corner)


def update(pos, head, side, g2, l21, own, wr, xs, w):
    rows, cols = w.shape
    steps = pl.cdiv(cols, TILE)
    whole = lambda a: pl.BlockSpec(a.shape, lambda i: (0,) * a.ndim)
    hbm = pl.BlockSpec(memory_space=pl.ANY)
    return pl.pallas_call(
        update_kernel,
        grid=(1,),
        out_shape=jax.ShapeDtypeStruct((rows, 1, 1, cols), F32),
        in_specs=[pl.BlockSpec(memory_space=pltpu.SMEM)] * 2
        + [whole(a) for a in (head, side, g2, l21, own, wr)]
        + [hbm] * (len(xs) + 1),
        out_specs=hbm,
        scratch_shapes=[
            pltpu.VMEM((steps, T, TILE), BF16),
            pltpu.VMEM((rows, cols), BF16),
            pltpu.VMEM((rows, 1, 1, cols), F32),
            pltpu.VMEM((pl.cdiv(rows, LANE), T, LANE), F32),
            pltpu.VMEM((TILE // LANE, T, LANE), F32),
            pltpu.SemaphoreType.DMA((steps, len(xs))),
            pltpu.SemaphoreType.DMA,
            pltpu.SemaphoreType.DMA((steps,)),
        ],
        compiler_params=pltpu.CompilerParams(vmem_limit_bytes=32 << 20),
        name="update",
    )(*pos, head, side, g2, l21, own, wr, *xs, w)


def everyone(x, axis, count):
    return lax.all_to_all(jnp.broadcast_to(x[None], (count,) + x.shape), axis, 0, 0, tiled=True)


def spread(x, axis, count, shifts):
    parts = [lax.ppermute(x, axis, [(i, (i + d) % count) for i in range(count)]) for d in shifts]
    return [x] + parts


def on_device(kernel):
    work = kernel[:, 0, 0, :]
    rows, cols = work.shape
    r = lax.axis_index(("y", "zh", "zl"))
    q = lax.axis_index(("x", "c"))
    pos = (r.reshape(1).astype(jnp.int32), q.reshape(1).astype(jnp.int32))
    head_rows = jnp.pad(work[0:LR, :], ((0, 0), (0, -cols % LANE)))

    wr = everyone(jnp.transpose(work[:, 0:LC]), ("x", "c"), COLS).reshape(T, rows)

    x = jnp.concatenate(spread(head_rows, ("zh", "zl"), NZ, FAR), axis=0)
    across = spread(x, "y", NY, NEAR[2:])[1]
    x = jnp.concatenate(spread(x, ("zh", "zl"), NZ, NEAR), axis=0)
    x, wr = lax.optimization_barrier((x, wr))
    pieces = jnp.broadcast_to(jnp.transpose(x[:, 0:LC])[None], (NY * COLS, LC, NZ * LR))
    x, across, pieces = lax.optimization_barrier((x, across, pieces))
    corner = lax.all_to_all(pieces, ("y", "x", "c"), 0, 0, tiled=True).reshape(NY, T, NZ * LR)
    xs = spread(x, "y", NY, NEAR[:2]) + spread(across, ("zh", "zl"), NZ, NEAR)

    head, side, g2, l21, own = factor(pos, corner)
    return update(pos, head, side, g2, l21, own, wr, xs, work)


def solution(mesh):
    inner = Mesh(mesh.devices.reshape(NY, NZH, NZL, NX, NC), ("y", "zh", "zl", "x", "c"))
    spec = P(None, ("y", "zh", "zl"), ("x", "c"), None)
    return jax.shard_map(on_device, mesh=inner, in_specs=(spec,), out_specs=spec, check_vma=False)
```
